32 devices in a mesh: gx: 8 (over z, x), gy: 4 (over y, core).
Axes of the slice: x: 2, y: 2, z: 4, core: 2. Of those that a mesh axis runs over, the one named last changes fastest.
Arguments:
- site_frac: float32 [3, 16, 8, 128], P(None, 'gx', 'gy'), may hold values from 0 to 1
- dual_weight: float32 [16, 8, 128], P('gx', 'gy'), may hold values from -2.5 to 64
- target_mass: float32 [16, 8, 128], P('gx', 'gy'), may hold values from 0.2 to 0.8
- block_list: int32 [8, 4, 12], P('gx', 'gy'), may hold values from 0 to 35, as said below
- block_count: int32 [8, 4], P('gx', 'gy'), may hold values from 1 to 12, as said below
Outputs:
- new_dual: float32 [16, 8, 128], P('gx', 'gy')
- site_shift: float32 [3, 16, 8, 128], P(None, 'gx', 'gy')
- displacement: float32 [3, 32, 16, 256], P(None, 'gx', 'gy')
The draws below stay inside these ranges and needn't reach their ends.
Inputs may be any that keep to these rules, and one draw needn't show every extreme that they name: `block_list`: within one tile the 12 entries are distinct. The first block_count entries name halo slots whose blocks hold sites of that tile's neighbourhood. `block_count`: some tile uses all 12 entries.
All inputs are finite; a program needn't handle non-finite values.
Results may differ from the reference program's by a relative error of at most 0.0003.
Values sent between devices are 32-bit elements; how exact they have to be, the bound alone decides.
A program may use at most 64 MiB of HBM per device.

```python
import jax
import jax.numpy as jnp
from jax import lax

TX = 4
TY = 4
Z = 256
SB_SIDE = 2
BLOCK = 128
K_MAX = 12
NBX = 16
NBY = 8
NX = 32
NY = 16
N_GX = 8
N_GY = 4


def layout_draw(key):
    base_key = jax.random.fold_in(key, 11)
    key_first = jax.random.fold_in(base_key, 0)
    key_pick = jax.random.fold_in(base_key, 2)
    key_order = jax.random.fold_in(base_key, 3)
    blocks = SB_SIDE * SB_SIDE
    lowest = blocks // 2
    living = jax.random.randint(key_first, (N_GX, N_GY), lowest, blocks + 1)
    chosen_tile = jax.random.randint(key_pick, (), 0, N_GX * N_GY)
    tile_serial = jnp.arange(N_GX * N_GY).reshape(N_GX, N_GY)
    living = jnp.where(tile_serial == chosen_tile, blocks, living)
    span_slots = 3 * SB_SIDE
    slot_ids = jnp.arange(span_slots * span_slots)
    slot_row = slot_ids // span_slots
    slot_col = slot_ids % span_slots
    near_x = (jnp.arange(N_GX)[:, None, None] + slot_row[None, None, :] // SB_SIDE - 1) % N_GX
    near_y = (jnp.arange(N_GY)[None, :, None] + slot_col[None, None, :] // SB_SIDE - 1) % N_GY
    inner_id = slot_row % SB_SIDE * SB_SIDE + slot_col % SB_SIDE
    usable = (inner_id[None, None, :] < living[near_x, near_y]).astype(jnp.int32)
    ranking = jax.random.randint(key_order, (N_GX, N_GY, span_slots * span_slots), 0, 1024)
    keyed_rank = usable * (1024 * span_slots * span_slots) + ranking * (span_slots * span_slots) + slot_ids[None, None, :]
    ignored, chosen_order = lax.top_k(keyed_rank, K_MAX)
    available = jnp.sum(usable, axis=-1)
    counts = jnp.minimum(jnp.minimum(available, K_MAX), (K_MAX * living + blocks - 1) // blocks)
    return (chosen_order.astype(jnp.int32), counts.astype(jnp.int32))


def draw_block_list(key, part):
    return layout_draw(key)[0]


def draw_block_count(key, part):
    return layout_draw(key)[1]


def draw_dual_weight(key, part):
    key_base = jax.random.fold_in(jax.random.fold_in(key, 23), 0)
    dims_shape = (NBX, NBY, BLOCK)
    return jnp.clip(0.5 * jax.random.normal(key_base, dims_shape, jnp.float32), -2.5, 2.5)


def block_levels(own_key, extent, cuts, least, largest):
    level, own = 1.0, jax.random.fold_in(own_key, 6)
    for dim, blocks in cuts:
        draws = jnp.exp(jax.random.uniform(jax.random.fold_in(own, dim), (blocks,), jnp.float32, least / len(cuts), largest / len(cuts)))
        level = level * jnp.repeat(draws, extent[dim] // blocks).reshape([-1 if axis == dim else 1 for axis in range(len(extent))])
    return level


def setup_inputs(seed: int = 0) -> dict:
    keys = jax.random.split(jax.random.key(seed), 6)
    site_frac = jnp.clip(1.0 * jax.random.uniform(keys[0], (3, NBX, NBY, BLOCK), jnp.float32) ** block_levels(keys[0], (3, NBX, NBY, BLOCK), ((1, 8), (2, 4)), -0.2, 0.2), 0.0, 1.0)
    dual_weight = draw_dual_weight(jax.random.fold_in(keys[5], 71), 0)
    target_mass = jnp.clip(0.2 + 0.6 * jax.random.uniform(keys[2], (NBX, NBY, BLOCK), jnp.float32) ** block_levels(keys[2], (NBX, NBY, BLOCK), ((0, 8), (1, 4)), -0.2, 0.2), 0.2, 0.8)
    block_list = draw_block_list(jax.random.fold_in(keys[5], 71), 0)
    block_count = draw_block_count(jax.random.fold_in(keys[5], 71), 0)
    return {"site_frac": site_frac, "dual_weight": dual_weight, "target_mass": target_mass, "block_list": block_list, "block_count": block_count}


entropy_scale = 0.5
step_rate = 0.5


def grid_points(first_row, how_many):
    serial = first_row + jnp.arange(how_many)
    cell_x = serial // (TY * Z)
    cell_y = (serial // Z) % TY
    cell_z = serial % Z
    return jnp.stack([cell_x, cell_y, cell_z]).astype(jnp.float32) + 0.5


def assign(points, chosen, usable, moments):
    spread = points[:, :, None] - chosen[:3, None, :]
    distance = spread[0] * spread[0] + spread[1] * spread[1] + spread[2] * spread[2]
    scores = jnp.where(usable[None, :], (chosen[3][None, :] - distance) / entropy_scale, -jnp.inf)
    peak_score = jnp.max(scores, axis=1, keepdims=True)
    weights = jnp.exp(scores - peak_score)
    shares = weights / jnp.sum(weights, axis=1, keepdims=True)
    masses = jnp.sum(shares, axis=0)
    if not moments:
        return masses, None, None
    moment = jnp.sum(shares[None] * spread, axis=1)
    offsets = -jnp.sum(shares[None] * spread, axis=2)
    return masses, moment, offsets


def wrapped(tile_pos, total_blocks):
    return (tile_pos * SB_SIDE - SB_SIDE + jnp.arange(3 * SB_SIDE)) % total_blocks


def tile_step(site_frac, duals, block_list, block_count, tile_id):
    tile_x = tile_id // N_GY
    tile_y = tile_id % N_GY
    row_ids = wrapped(tile_x, NBX)
    col_ids = wrapped(tile_y, NBY)
    fraction = site_frac[:, row_ids][:, :, col_ids]
    local_duals = duals[row_ids][:, col_ids]
    offset = (jnp.arange(3 * SB_SIDE) // SB_SIDE - 1).astype(jnp.float32)
    site_table = jnp.stack([fraction[0] * TX + offset[:, None, None] * TX,
                            fraction[1] * TY + offset[None, :, None] * TY,
                            fraction[2] * Z, local_duals])
    flat_table = site_table.reshape(4, 9 * SB_SIDE * SB_SIDE, BLOCK)
    chosen_ids = block_list[tile_x, tile_y]
    live_count = block_count[tile_x, tile_y]
    chosen = flat_table[:, chosen_ids].reshape(4, K_MAX * BLOCK)
    usable = jnp.arange(K_MAX * BLOCK) // BLOCK < live_count
    masses, moment, offsets = assign(grid_points(0, TX * TY * Z), chosen, usable, True)
    partials = jnp.concatenate([masses[None], moment], 0).reshape(4, K_MAX, BLOCK)
    partials = jnp.where((jnp.arange(K_MAX) < live_count)[None, :, None], partials, 0.0)
    summed = jnp.zeros((4, 9 * SB_SIDE * SB_SIDE, BLOCK), jnp.float32).at[:, chosen_ids].add(partials)
    return summed, offsets


def one_step(site_frac, duals, block_list, block_count):
    tile_total = N_GX * N_GY
    summed, offsets = lax.map(lambda tile_id: tile_step(site_frac, duals, block_list, block_count, tile_id),
                              jnp.arange(tile_total))
    tile_serial = jnp.arange(tile_total)
    row_ids = ((tile_serial // N_GY)[:, None] * SB_SIDE - SB_SIDE + jnp.arange(3 * SB_SIDE)[None, :]) % NBX
    col_ids = ((tile_serial % N_GY)[:, None] * SB_SIDE - SB_SIDE + jnp.arange(3 * SB_SIDE)[None, :]) % NBY
    pieces = summed.reshape(tile_total, 4, 3 * SB_SIDE, 3 * SB_SIDE, BLOCK).transpose(0, 2, 3, 1, 4)
    totals = jnp.zeros((NBX, NBY, 4, BLOCK), jnp.float32).at[row_ids[:, :, None], col_ids[:, None, :]].add(pieces)
    return totals.transpose(2, 0, 1, 3), offsets


def reference(site_frac, dual_weight, target_mass, block_list, block_count):
    totals, offsets = one_step(site_frac, dual_weight, block_list, block_count)
    dual_mid = dual_weight + step_rate * (target_mass - totals[0])
    totals, offsets = one_step(site_frac, dual_mid, block_list, block_count)
    new_dual = dual_mid + step_rate * (target_mass - totals[0])
    site_shift = totals[1:] / (totals[0] + target_mass)[None]
    displacement = offsets.reshape(N_GX, N_GY, 3, TX, TY, Z).transpose(2, 0, 3, 1, 4, 5).reshape(3, NX, NY, Z)
    return new_dual, site_shift, displacement
```

```python
import functools
import math

import jax
import jax.numpy as jnp
from jax import lax
from jax.experimental import pallas as pl
from jax.experimental.pallas import tpu as pltpu
from jax.sharding import PartitionSpec as P

TX = 4
TY = 4
Z = 256

entropy_scale = 0.5
step_rate = 0.5

SCALE = 1.0 / (entropy_scale * math.log(2.0))
DEAD = -1e30
CHUNK = 16
AROUND = [d for d in range(9) if d != 4]
QUADS = [(a, b) for a in range(TX // 2) for b in range(TY // 2)]
NT = (((1,), (1,)), ((), ()))
NN = (((1,), (0,)), ((), ()))


def halves(value):
    high = value.astype(jnp.bfloat16)
    low = (value - high.astype(jnp.float32)).astype(jnp.bfloat16)
    return high, low


def product(pair, high, low, dims):
    rows = pair.shape[0] // 2
    both = lax.dot_general(pair, high, dims, preferred_element_type=jnp.float32)
    rest = lax.dot_general(pair[:rows], low, dims, preferred_element_type=jnp.float32)
    return both[:rows] + both[rows:] + rest


def kernel(
    frac_ref, dual_ref, target_ref, list_ref, count_ref,
    new_ref, shift_ref, disp_ref,
    frac_all, dual_all, mid_all, part_send, part_recv, four_send, four_recv,
    table, base_ref, plain_pair, terms, terms_pair,
    g_high, g_low, gz_high, gz_low, send_sem, recv_sem,
):
    side = frac_ref.shape[1]
    block = frac_ref.shape[3]
    slots = list_ref.shape[2]
    columns = slots * block
    span = 3 * side
    gx, gy = lax.axis_index("gx"), lax.axis_index("gy")
    nx, ny = lax.axis_size("gx"), lax.axis_size("gy")

    def device(d):
        return (lax.rem(gx + d // 3 - 1 + nx, nx), lax.rem(gy + d % 3 - 1 + ny, ny))

    def copy(phase, d, src, dst):
        return pltpu.make_async_remote_copy(
            src_ref=src, dst_ref=dst.at[8 - d],
            send_sem=send_sem.at[phase, d], recv_sem=recv_sem.at[phase, 8 - d],
            device_id=device(d), device_id_type=pl.DeviceIdType.MESH,
        )

    def finish(copies):
        for one in copies:
            one.wait()

    barrier = pltpu.get_barrier_semaphore()
    for d in AROUND:
        pl.semaphore_signal(
            barrier, inc=1, device_id=device(d), device_id_type=pl.DeviceIdType.MESH
        )
    pl.semaphore_wait(barrier, len(AROUND))

    first = [copy(0, d, frac_ref, frac_all) for d in AROUND]
    first += [copy(1, d, dual_ref, dual_all) for d in AROUND]
    for one in first:
        one.start()
    frac_all[4] = frac_ref[...]
    dual_all[4] = dual_ref[...]
    finish(first)

    ids = [list_ref[0, 0, m] for m in range(slots)]
    live = count_ref[0, 0]
    places = []
    for m in range(slots):
        row, col = ids[m] // span, ids[m] % span
        tile_x, tile_y = row // side, col // side
        places.append((tile_x * 3 + tile_y, row % side, col % side))
        at = slice(m * block, (m + 1) * block)
        where = (places[m][1], places[m][2])
        table[0:1, at] = (
            frac_all[places[m][0], 0, where[0], pl.ds(where[1], 1), :] * TX
            + (tile_x - 1).astype(jnp.float32) * TX
        )
        table[1:2, at] = (
            frac_all[places[m][0], 1, where[0], pl.ds(where[1], 1), :] * TY
            + (tile_y - 1).astype(jnp.float32) * TY
        )
        table[2:3, at] = frac_all[places[m][0], 2, where[0], pl.ds(where[1], 1), :] * Z

    def load_duals(source):
        for m in range(slots):
            row = source[places[m][0], places[m][1], pl.ds(places[m][2], 1), :]
            table[3:4, m * block : (m + 1) * block] = jnp.where(m < live, row * SCALE, DEAD)

    load_duals(dual_all)

    serial = lax.broadcasted_iota(jnp.int32, (16, columns), 0)
    kind = serial % 4
    step_x = (serial // 8).astype(jnp.float32) - 0.5
    step_y = (serial // 4 % 2).astype(jnp.float32) - 0.5
    for n, (a, b) in enumerate(QUADS):
        centre_x = (2 * a + 1.0) - table[0:1, :]
        centre_y = (2 * b + 1.0) - table[1:2, :]
        base_ref[n : n + 1, :] = -SCALE * (centre_x * centre_x + centre_y * centre_y)
        plain = jnp.exp2((-2.0 * SCALE) * (step_x * centre_x + step_y * centre_y))
        factor = jnp.where(kind == 1, centre_x + step_x, jnp.where(kind == 2, centre_y + step_y, 1.0))
        with_factor = plain * factor
        terms[n] = with_factor
        high, low = halves(plain)
        plain_pair[n, :16] = high
        plain_pair[n, 16:] = low
        high, low = halves(with_factor)
        terms_pair[n, :16] = high
        terms_pair[n, 16:] = low

    def build(with_moments):
        levels = [base_ref[n : n + 1, :] + table[3:4, :] for n in range(len(QUADS))]

        def chunk(c, carry):
            start = pl.multiple_of(c * CHUNK, CHUNK)
            z = lax.broadcasted_iota(jnp.int32, (CHUNK, columns), 0) + start
            dz = (z.astype(jnp.float32) + 0.5) - table[2:3, :]
            depth = dz * dz * (-SCALE)
            for n in range(len(QUADS)):
                score = depth + levels[n]
                g = jnp.exp2(score - jnp.max(score, axis=1, keepdims=True))
                high, low = halves(g)
                g_high[n, pl.ds(start, CHUNK), :] = high
                g_low[n, pl.ds(start, CHUNK), :] = low
                if with_moments:
                    high, low = halves(g * dz)
                    gz_high[n, pl.ds(start, CHUNK), :] = high
                    gz_low[n, pl.ds(start, CHUNK), :] = low
            return carry

        lax.fori_loop(0, Z // CHUNK, chunk, 0)

    def fold_rows(total):
        eight = total[:8] + total[8:]
        return eight + pltpu.roll(eight, 4, 0)

    shape = (side, side, block)
    inner = lax.broadcasted_iota(jnp.int32, shape, 0) * side + lax.broadcasted_iota(
        jnp.int32, shape, 1
    )

    def place(rows, kind_index, d):
        found = jnp.zeros(shape, jnp.float32)
        for m in range(slots):
            value = rows[kind_index : kind_index + 1, m * block : (m + 1) * block]
            wanted = places[m][1] * side + places[m][2] + (side * side) * (places[m][0] - d)
            found = found + jnp.where(
                inner == wanted, jnp.broadcast_to(value[None], shape), 0.0
            )
        return found

    build(False)
    total = jnp.zeros((16, columns), jnp.float32)
    for n in range(len(QUADS)):
        sums = product(plain_pair[n], g_high[n], g_low[n], NT)
        pair = jnp.concatenate(halves(1.0 / sums), axis=0)
        total = total + terms[n] * product(pair, g_high[n], g_low[n], NN)
    rows = fold_rows(total)
    for d in range(9):
        part_send[d] = place(rows, 0, d)
    second = [copy(2, d, part_send.at[d], part_recv) for d in AROUND]
    for one in second:
        one.start()
    finish(second)
    mass = part_send[4]
    for d in AROUND:
        mass = mass + part_recv[d]
    dual_mid = dual_ref[...] + step_rate * (target_ref[...] - mass)
    mid_all[4] = dual_mid
    third = [copy(3, d, mid_all.at[4], mid_all) for d in AROUND]
    for one in third:
        one.start()
    finish(third)

    load_duals(mid_all)
    build(True)
    total = jnp.zeros((16, columns), jnp.float32)
    is_z = kind == 3
    for n, (a, b) in enumerate(QUADS):
        sums = product(plain_pair[n], g_high[n], g_low[n], NT)
        inverse = 1.0 / sums
        pair = jnp.concatenate(halves(inverse), axis=0)
        masses = product(pair, g_high[n], g_low[n], NN)
        depths = product(pair, gz_high[n], gz_low[n], NN)
        total = total + terms[n] * jnp.where(is_z, depths, masses)
        across = product(terms_pair[n], g_high[n], g_low[n], NT)
        along = product(plain_pair[n], gz_high[n], gz_low[n], NT)
        offset = -inverse * jnp.where(is_z[:, :Z], along, across)
        for r in range(4):
            for c in range(3):
                disp_ref[c, 2 * a + r // 2, 2 * b + r % 2 : 2 * b + r % 2 + 1, :] = offset[
                    4 * r + c + 1 : 4 * r + c + 2, :
                ]
    rows = fold_rows(total)
    for d in range(9):
        for c in range(4):
            four_send[d, c] = place(rows, c, d)
    fourth = [copy(4, d, four_send.at[d], four_recv) for d in AROUND]
    for one in fourth:
        one.start()
    finish(fourth)
    four = four_send[4]
    for d in AROUND:
        four = four + four_recv[d]
    new_ref[...] = dual_mid + step_rate * (target_ref[...] - four[0])
    weight = 1.0 / (four[0] + target_ref[...])
    for c in range(3):
        shift_ref[c] = four[c + 1] * weight


def on_device(site_frac, dual_weight, target_mass, block_list, block_count):
    side = site_frac.shape[1]
    block = site_frac.shape[3]
    columns = block_list.shape[2] * block
    quads = len(QUADS)
    f32, bf16 = jnp.float32, jnp.bfloat16
    vmem = pl.BlockSpec(memory_space=pltpu.VMEM)
    smem = pl.BlockSpec(memory_space=pltpu.SMEM)
    return pl.pallas_call(
        kernel,
        out_shape=(
            jax.ShapeDtypeStruct(dual_weight.shape, f32),
            jax.ShapeDtypeStruct(site_frac.shape, f32),
            jax.ShapeDtypeStruct((3, TX, TY, Z), f32),
        ),
        in_specs=[vmem, vmem, vmem, smem, smem],
        out_specs=(vmem, vmem, vmem),
        scratch_shapes=[
            pltpu.VMEM((9,) + site_frac.shape, f32),
            pltpu.VMEM((9,) + dual_weight.shape, f32),
            pltpu.VMEM((9,) + dual_weight.shape, f32),
            pltpu.VMEM((9, side, side, block), f32),
            pltpu.VMEM((9, side, side, block), f32),
            pltpu.VMEM((9, 4, side, side, block), f32),
            pltpu.VMEM((9, 4, side, side, block), f32),
            pltpu.VMEM((8, columns), f32),
            pltpu.VMEM((8, columns), f32),
            pltpu.VMEM((quads, 32, columns), bf16),
            pltpu.VMEM((quads, 16, columns), f32),
            pltpu.VMEM((quads, 32, columns), bf16),
            pltpu.VMEM((quads, Z, columns), bf16),
            pltpu.VMEM((quads, Z, columns), bf16),
            pltpu.VMEM((quads, Z, columns), bf16),
            pltpu.VMEM((quads, Z, columns), bf16),
            pltpu.SemaphoreType.DMA((5, 9)),
            pltpu.SemaphoreType.DMA((5, 9)),
        ],
        compiler_params=pltpu.CompilerParams(collective_id=0, has_side_effects=True),
        name="transport",
    )(site_frac, dual_weight, target_mass, block_list, block_count)


def solution(mesh):
    in_specs = (
        P(None, "gx", "gy", None),
        P("gx", "gy", None),
        P("gx", "gy", None),
        P("gx", "gy", None),
        P("gx", "gy"),
    )
    out_specs = (P("gx", "gy", None), P(None, "gx", "gy", None), P(None, "gx", "gy", None))
    return jax.shard_map(
        on_device, mesh=mesh, in_specs=in_specs, out_specs=out_specs, check_vma=False
    )
```

```python
import functools
import math

import jax
import jax.numpy as jnp
from jax import lax
from jax.experimental import pallas as pl
from jax.experimental.pallas import tpu as pltpu
from jax.sharding import PartitionSpec as P

TX = 4
TY = 4
Z = 256

entropy_scale = 0.5
step_rate = 0.5

SCALE = 1.0 / (entropy_scale * math.log(2.0))
DEAD = -1e30
LIFT = 40.0
HEAD = 2.0**30
UNIT_XY = 8.0
UNIT_Z = float(Z)
CHUNK = 16
AROUND = [d for d in range(9) if d != 4]
GROUPS = TX // 2
ROWS = 2 * TY * 4
NT = (((1,), (1,)), ((), ()))
NN = (((1,), (0,)), ((), ()))


def halves(value):
    high = value.astype(jnp.bfloat16)
    low = (value - high.astype(jnp.float32)).astype(jnp.bfloat16)
    return high, low


def product(pair, high, low, dims):
    rows = pair.shape[0] // 2
    both = lax.dot_general(pair, high, dims, preferred_element_type=jnp.float32)
    rest = lax.dot_general(pair[:rows], low, dims, preferred_element_type=jnp.float32)
    return both[:rows] + both[rows:] + rest


def kernel(
    frac_ref, dual_ref, target_ref, list_ref, count_ref,
    new_ref, shift_ref, disp_ref,
    frac_all, dual_all, target, mid_all, part_send, part_recv, four_send, four_recv,
    list_held, count_held, table, base_ref, plain_rows, plain_pair, terms, terms_pair,
    inverses, g_high, g_low, gz_high, gz_low, disp_held, send_sem, recv_sem, local_sem,
):
    side = frac_ref.shape[1]
    block = frac_ref.shape[3]
    slots = list_ref.shape[2]
    columns = slots * block
    span = 3 * side
    gx, gy = lax.axis_index("gx"), lax.axis_index("gy")
    nx, ny = lax.axis_size("gx"), lax.axis_size("gy")

    def device(d):
        return (lax.rem(gx + d // 3 - 1 + nx, nx), lax.rem(gy + d % 3 - 1 + ny, ny))

    def copy(phase, d, src, dst):
        return pltpu.make_async_remote_copy(
            src_ref=src, dst_ref=dst.at[8 - d],
            send_sem=send_sem.at[phase, d], recv_sem=recv_sem.at[phase, 8 - d],
            device_id=device(d), device_id_type=pl.DeviceIdType.MESH,
        )

    def begin(copies):
        for one in copies:
            one.start()
        return copies

    def finish(copies):
        for one in copies:
            one.wait()

    barrier = pltpu.get_barrier_semaphore()
    for d in AROUND:
        pl.semaphore_signal(
            barrier, inc=1, device_id=device(d), device_id_type=pl.DeviceIdType.MESH
        )
    finish(begin([
        pltpu.make_async_copy(src, dst, local_sem.at[n])
        for n, (src, dst) in enumerate([
            (frac_ref, frac_all.at[4]), (dual_ref, dual_all.at[4]), (target_ref, target),
            (list_ref, list_held), (count_ref, count_held),
        ])
    ]))
    live = count_held[0, 0]
    places = []
    for m in range(slots):
        slot = list_held[0, 0, m]
        row, col = slot // span, slot % span
        places.append(((row // side) * 3 + col // side, row % side, col % side,
                       (row // side - 1).astype(jnp.float32) * TX,
                       (col // side - 1).astype(jnp.float32) * TY))
    pl.semaphore_wait(barrier, len(AROUND))

    finish(begin(
        [copy(0, d, frac_all.at[4], frac_all) for d in AROUND]
        + [copy(1, d, dual_all.at[4], dual_all) for d in AROUND]
    ))

    for m in range(slots):
        tile, row, col, corner_x, corner_y = places[m]
        at = slice(m * block, (m + 1) * block)
        table[0:1, at] = frac_all[tile, 0, row, pl.ds(col, 1), :] * TX + corner_x
        table[1:2, at] = frac_all[tile, 1, row, pl.ds(col, 1), :] * TY + corner_y
        table[2:3, at] = frac_all[tile, 2, row, pl.ds(col, 1), :] * Z

    def load_duals(source):
        for m in range(slots):
            row = source[places[m][0], places[m][1], pl.ds(places[m][2], 1), :]
            table[3:4, m * block : (m + 1) * block] = jnp.where(m < live, row * SCALE, DEAD)

    load_duals(dual_all)

    serial = lax.broadcasted_iota(jnp.int32, (ROWS, columns), 0)
    kind = serial % 4
    step_x = (serial // (4 * TY)).astype(jnp.float32) - 0.5
    step_y = (serial // 4 % TY).astype(jnp.float32) - 0.5 * (TY - 1)

    def centres(n):
        return (2 * n + 1.0) - table[0:1, :], 0.5 * TY - table[1:2, :]

    for n in range(GROUPS):
        centre_x, centre_y = centres(n)
        base_ref[n : n + 1, :] = -SCALE * (centre_x * centre_x + centre_y * centre_y)
        plain = jnp.exp2((-2.0 * SCALE) * (step_x * centre_x + step_y * centre_y))
        plain_rows[n] = plain
        high, low = halves(plain)
        plain_pair[n, :ROWS] = high
        plain_pair[n, ROWS:] = low

    def build(with_moments):
        levels = [base_ref[n : n + 1, :] + table[3:4, :] for n in range(GROUPS)]

        def chunk(c, carry):
            start = pl.multiple_of(c * CHUNK, CHUNK)
            z = lax.broadcasted_iota(jnp.int32, (CHUNK, columns), 0) + start
            dz = (z.astype(jnp.float32) + 0.5) - table[2:3, :]
            depth = dz * dz * (-SCALE)
            for n in range(GROUPS):
                score = depth + levels[n]
                g = jnp.exp2(score - (jnp.max(score, axis=1, keepdims=True) - LIFT))
                high, low = halves(g)
                g_high[n, pl.ds(start, CHUNK), :] = high
                g_low[n, pl.ds(start, CHUNK), :] = low
                if with_moments:
                    high, low = halves(g * (dz * (1.0 / UNIT_Z)))
                    gz_high[n, pl.ds(start, CHUNK), :] = high
                    gz_low[n, pl.ds(start, CHUNK), :] = low
            return carry

        lax.fori_loop(0, Z // CHUNK, chunk, 0, unroll=2)

    def invert(n):
        return HEAD / product(plain_pair[n], g_high[n], g_low[n], NT)

    def fold_rows(total):
        eight = total[:8]
        for r in range(8, ROWS, 8):
            eight = eight + total[r : r + 8]
        return eight + pltpu.roll(eight, 4, 0)

    build(False)
    pairs = [jnp.concatenate(halves(invert(n)), axis=0) for n in range(GROUPS)]
    total = jnp.zeros((ROWS, columns), jnp.float32)
    for n in range(GROUPS):
        total = total + plain_rows[n] * product(pairs[n], g_high[n], g_low[n], NN)
    rows = fold_rows(total) * (1.0 / HEAD)
    shape = (side, side, block)
    inner = lax.broadcasted_iota(jnp.int32, shape, 0) * side + lax.broadcasted_iota(
        jnp.int32, shape, 1
    )
    wanted = [places[m][1] * side + places[m][2] + (side * side) * places[m][0] for m in range(slots)]
    spread = [
        jnp.broadcast_to(rows[0:1, m * block : (m + 1) * block][None], shape) for m in range(slots)
    ]
    for d in range(9):
        found = jnp.zeros(shape, jnp.float32)
        for m in range(slots):
            found = found + jnp.where(inner == wanted[m] - side * side * d, spread[m], 0.0)
        part_send[d] = found
    second = begin([copy(2, d, part_send.at[d], part_recv) for d in AROUND])
    for n in range(GROUPS):
        centre_x, centre_y = centres(n)
        across = (centre_x + step_x) * (1.0 / UNIT_XY)
        aside = (centre_y + step_y) * (1.0 / UNIT_XY)
        factor = jnp.where(kind == 1, across, jnp.where(kind == 2, aside, 1.0))
        with_factor = plain_rows[n] * factor
        terms[n] = with_factor
        high, low = halves(with_factor)
        terms_pair[n, :ROWS] = high
        terms_pair[n, ROWS:] = low
    finish(second)
    mass = part_send[4]
    for d in AROUND:
        mass = mass + part_recv[d]
    dual_mid = dual_all[4] + step_rate * (target[...] - mass)
    mid_all[4] = dual_mid
    finish(begin([copy(3, d, mid_all.at[4], mid_all) for d in AROUND]))

    load_duals(mid_all)
    build(True)
    pairs = []
    for n in range(GROUPS):
        inverse = invert(n)
        inverses[n] = inverse
        pairs.append(jnp.concatenate(halves(inverse), axis=0))
    total = jnp.zeros((ROWS, columns), jnp.float32)
    for n in range(GROUPS):
        masses = product(pairs[n], g_high[n], g_low[n], NN)
        depths = product(pairs[n], gz_high[n], gz_low[n], NN)
        total = total + terms[n] * jnp.where(kind == 3, depths, masses)

    def units(shape):
        which = lax.broadcasted_iota(jnp.int32, shape, 0) % 4
        unit = jnp.where(which == 0, 1.0, jnp.where(which == 3, UNIT_Z, UNIT_XY))
        return unit * (1.0 / HEAD)

    rows = fold_rows(total) * units((8, columns))
    half = lax.broadcasted_iota(jnp.int32, (8, block), 0) // 4
    for d in range(9):
        for v in range(side * side // 2):
            found = jnp.zeros((8, block), jnp.float32)
            for m in range(slots):
                here = half == wanted[m] - (side * side * d + 2 * v)
                found = found + jnp.where(here, rows[:, m * block : (m + 1) * block], 0.0)
            four_send[d, 8 * v : 8 * v + 8, :] = found
    fourth = begin([copy(4, d, four_send.at[d], four_recv) for d in AROUND])
    scale = -units((ROWS, Z))
    is_z = lax.broadcasted_iota(jnp.int32, (ROWS, Z), 0) % 4 == 3
    for n in range(GROUPS):
        across = product(terms_pair[n], g_high[n], g_low[n], NT)
        along = product(plain_pair[n], gz_high[n], gz_low[n], NT)
        offset = (inverses[n] * jnp.where(is_z, along, across)) * scale
        for r in range(2 * TY):
            for c in range(3):
                disp_held[c, 2 * n + r // TY, r % TY : r % TY + 1, :] = offset[
                    4 * r + c + 1 : 4 * r + c + 2, :
                ]
    out = begin([pltpu.make_async_copy(disp_held, disp_ref, local_sem.at[5])])
    finish(fourth)
    four = four_send[4]
    for d in AROUND:
        four = four + four_recv[d]
    for i in range(side * side):
        r, c = i // side, i % side
        goal = target[r, c : c + 1, :]
        found = four[4 * i : 4 * i + 1]
        new_ref[r, c : c + 1, :] = mid_all[4, r, c : c + 1, :] + step_rate * (goal - found)
        weight = 1.0 / (found + goal)
        for k in range(3):
            shift_ref[k, r, c : c + 1, :] = four[4 * i + k + 1 : 4 * i + k + 2] * weight
    finish(out)


def on_device(site_frac, dual_weight, target_mass, block_list, block_count):
    side = site_frac.shape[1]
    block = site_frac.shape[3]
    columns = block_list.shape[2] * block
    f32, bf16, i32 = jnp.float32, jnp.bfloat16, jnp.int32
    vmem = pl.BlockSpec(memory_space=pltpu.VMEM)
    place = pl.BlockSpec(memory_space=pl.ANY)
    return pl.pallas_call(
        kernel,
        out_shape=(
            jax.ShapeDtypeStruct(dual_weight.shape, f32),
            jax.ShapeDtypeStruct(site_frac.shape, f32),
            jax.ShapeDtypeStruct((3, TX, TY, Z), f32),
        ),
        in_specs=[place] * 5,
        out_specs=(vmem, vmem, place),
        scratch_shapes=[
            pltpu.VMEM((9,) + site_frac.shape, f32),
            pltpu.VMEM((9,) + dual_weight.shape, f32),
            pltpu.VMEM(target_mass.shape, f32),
            pltpu.VMEM((9,) + dual_weight.shape, f32),
            pltpu.VMEM((9, side, side, block), f32),
            pltpu.VMEM((9, side, side, block), f32),
            pltpu.VMEM((9, 4 * side * side, block), f32),
            pltpu.VMEM((9, 4 * side * side, block), f32),
            pltpu.SMEM(block_list.shape, i32),
            pltpu.SMEM(block_count.shape, i32),
            pltpu.VMEM((8, columns), f32),
            pltpu.VMEM((8, columns), f32),
            pltpu.VMEM((GROUPS, ROWS, columns), f32),
            pltpu.VMEM((GROUPS, 2 * ROWS, columns), bf16),
            pltpu.VMEM((GROUPS, ROWS, columns), f32),
            pltpu.VMEM((GROUPS, 2 * ROWS, columns), bf16),
            pltpu.VMEM((GROUPS, ROWS, Z), f32),
            pltpu.VMEM((GROUPS, Z, columns), bf16),
            pltpu.VMEM((GROUPS, Z, columns), bf16),
            pltpu.VMEM((GROUPS, Z, columns), bf16),
            pltpu.VMEM((GROUPS, Z, columns), bf16),
            pltpu.VMEM((3, TX, TY, Z), f32),
            pltpu.SemaphoreType.DMA((5, 9)),
            pltpu.SemaphoreType.DMA((5, 9)),
            pltpu.SemaphoreType.DMA((6,)),
        ],
        compiler_params=pltpu.CompilerParams(collective_id=0, has_side_effects=True),
        name="transport",
    )(site_frac, dual_weight, target_mass, block_list, block_count)


def solution(mesh):
    in_specs = (
        P(None, "gx", "gy", None),
        P("gx", "gy", None),
        P("gx", "gy", None),
        P("gx", "gy", None),
        P("gx", "gy"),
    )
    out_specs = (P("gx", "gy", None), P(None, "gx", "gy", None), P(None, "gx", "gy", None))
    return jax.shard_map(
        on_device, mesh=mesh, in_specs=in_specs, out_specs=out_specs, check_vma=False
    )
```

```python
import functools
import math

import jax
import jax.numpy as jnp
from jax import lax
from jax.experimental import pallas as pl
from jax.experimental.pallas import tpu as pltpu
from jax.sharding import PartitionSpec as P

TX = 4
TY = 4
Z = 256

entropy_scale = 0.5
step_rate = 0.5

SCALE = 1.0 / (entropy_scale * math.log(2.0))
DEAD = -1e30
LIFT = 40.0
HEAD = 2.0**30
UNIT_XY = 8.0
UNIT_Z = float(Z)
CHUNK = 16
AROUND = [d for d in range(9) if d != 4]
WIDE = [(a, b) for a in range(-2, 3) for b in range(-2, 3) if (a, b) != (0, 0)]
GROUPS = TX // 2
ROWS = 2 * TY * 4
NT = (((1,), (1,)), ((), ()))
NN = (((1,), (0,)), ((), ()))


def halves(value):
    high = value.astype(jnp.bfloat16)
    low = (value - high.astype(jnp.float32)).astype(jnp.bfloat16)
    return high, low


def product(pair, high, low, dims):
    rows = pair.shape[0] // 2
    both = lax.dot_general(pair, high, dims, preferred_element_type=jnp.float32)
    rest = lax.dot_general(pair[:rows], low, dims, preferred_element_type=jnp.float32)
    return both[:rows] + both[rows:] + rest


def kernel(
    frac_ref, dual_ref, target_ref, list_ref, count_ref,
    new_ref, shift_ref, disp_ref,
    frac_all, dual_all, target_all, mid_all, part_send, part_recv, four_send, four_recv,
    list_held, count_held, table, base_ref, plain_rows, plain_pair, terms, terms_pair,
    inverses, g_high, g_low, gz_high, gz_low, wide_send, wide_recv, send_sem, recv_sem, local_sem,
):
    side = frac_ref.shape[1]
    block = frac_ref.shape[3]
    slots = list_ref.shape[2]
    columns = slots * block
    span = 3 * side
    gx, gy = lax.axis_index("gx"), lax.axis_index("gy")
    nx, ny = lax.axis_size("gx"), lax.axis_size("gy")

    def device(d):
        return (lax.rem(gx + d // 3 - 1 + nx, nx), lax.rem(gy + d % 3 - 1 + ny, ny))

    def far(a, b):
        return (lax.rem(gx + a + nx, nx), lax.rem(gy + b + ny, ny))

    def wide_copy(a, b):
        here = tuple(pl.ds(max(v, 0), 3 - abs(v)) for v in (a, b))
        there = tuple(pl.ds(max(-v, 0), 3 - abs(v)) for v in (a, b))
        e = (a + 2) * 5 + b + 2
        return pltpu.make_async_remote_copy(
            src_ref=part_send.at[here], dst_ref=part_recv.at[(24 - e,) + there],
            send_sem=wide_send.at[e], recv_sem=wide_recv.at[24 - e],
            device_id=far(a, b), device_id_type=pl.DeviceIdType.MESH,
        )

    def copy(phase, d, src, dst):
        return pltpu.make_async_remote_copy(
            src_ref=src, dst_ref=dst.at[8 - d],
            send_sem=send_sem.at[phase, d], recv_sem=recv_sem.at[phase, 8 - d],
            device_id=device(d), device_id_type=pl.DeviceIdType.MESH,
        )

    def begin(copies):
        for one in copies:
            one.start()
        return copies

    def finish(copies):
        for one in copies:
            one.wait()

    barrier = pltpu.get_barrier_semaphore()
    for a, b in WIDE:
        pl.semaphore_signal(
            barrier, inc=1, device_id=far(a, b), device_id_type=pl.DeviceIdType.MESH
        )
    finish(begin([
        pltpu.make_async_copy(src, dst, local_sem.at[n])
        for n, (src, dst) in enumerate([
            (frac_ref, frac_all.at[4]), (dual_ref, dual_all.at[4]), (target_ref, target_all.at[4]),
            (list_ref, list_held), (count_ref, count_held),
        ])
    ]))
    live = count_held[0, 0]
    places = []
    for m in range(slots):
        slot = list_held[0, 0, m]
        row, col = slot // span, slot % span
        places.append(((row // side) * 3 + col // side, row % side, col % side,
                       (row // side - 1).astype(jnp.float32) * TX,
                       (col // side - 1).astype(jnp.float32) * TY))
    pl.semaphore_wait(barrier, len(WIDE))

    first = begin([copy(0, d, frac_all.at[4], frac_all) for d in AROUND])
    first += begin([copy(1, d, dual_all.at[4], dual_all) for d in AROUND])
    goals = begin([copy(2, d, target_all.at[4], target_all) for d in AROUND])
    finish(first)

    for m in range(slots):
        tile, row, col, corner_x, corner_y = places[m]
        at = slice(m * block, (m + 1) * block)
        table[0:1, at] = frac_all[tile, 0, row, pl.ds(col, 1), :] * TX + corner_x
        table[1:2, at] = frac_all[tile, 1, row, pl.ds(col, 1), :] * TY + corner_y
        table[2:3, at] = frac_all[tile, 2, row, pl.ds(col, 1), :] * Z

    def load_duals(source):
        for m in range(slots):
            row = source[places[m][0], places[m][1], pl.ds(places[m][2], 1), :]
            table[3:4, m * block : (m + 1) * block] = jnp.where(m < live, row * SCALE, DEAD)

    load_duals(dual_all)

    serial = lax.broadcasted_iota(jnp.int32, (ROWS, columns), 0)
    kind = serial % 4
    step_x = (serial // (4 * TY)).astype(jnp.float32) - 0.5
    step_y = (serial // 4 % TY).astype(jnp.float32) - 0.5 * (TY - 1)

    def centres(n):
        return (2 * n + 1.0) - table[0:1, :], 0.5 * TY - table[1:2, :]

    for n in range(GROUPS):
        centre_x, centre_y = centres(n)
        base_ref[n : n + 1, :] = -SCALE * (centre_x * centre_x + centre_y * centre_y)
        plain = jnp.exp2((-2.0 * SCALE) * (step_x * centre_x + step_y * centre_y))
        plain_rows[n] = plain
        high, low = halves(plain)
        plain_pair[n, :ROWS] = high
        plain_pair[n, ROWS:] = low

    def build(with_moments):
        levels = [base_ref[n : n + 1, :] + table[3:4, :] for n in range(GROUPS)]

        def chunk(c, carry):
            start = pl.multiple_of(c * CHUNK, CHUNK)
            z = lax.broadcasted_iota(jnp.int32, (CHUNK, columns), 0) + start
            dz = (z.astype(jnp.float32) + 0.5) - table[2:3, :]
            depth = dz * dz * (-SCALE)
            for n in range(GROUPS):
                score = depth + levels[n]
                g = jnp.exp2(score - (jnp.max(score, axis=1, keepdims=True) - LIFT))
                high, low = halves(g)
                g_high[n, pl.ds(start, CHUNK), :] = high
                g_low[n, pl.ds(start, CHUNK), :] = low
                if with_moments:
                    high, low = halves(g * (dz * (1.0 / UNIT_Z)))
                    gz_high[n, pl.ds(start, CHUNK), :] = high
                    gz_low[n, pl.ds(start, CHUNK), :] = low
            return carry

        lax.fori_loop(0, Z // CHUNK, chunk, 0, unroll=2)

    def invert(n):
        return HEAD / product(plain_pair[n], g_high[n], g_low[n], NT)

    def fold_rows(total):
        eight = total[:8]
        for r in range(8, ROWS, 8):
            eight = eight + total[r : r + 8]
        return eight + pltpu.roll(eight, 4, 0)

    build(False)
    pairs = [jnp.concatenate(halves(invert(n)), axis=0) for n in range(GROUPS)]
    total = jnp.zeros((ROWS, columns), jnp.float32)
    for n in range(GROUPS):
        total = total + plain_rows[n] * product(pairs[n], g_high[n], g_low[n], NN)
    rows = fold_rows(total) * (1.0 / HEAD)
    shape = (side, side, block)
    inner = lax.broadcasted_iota(jnp.int32, shape, 0) * side + lax.broadcasted_iota(
        jnp.int32, shape, 1
    )
    wanted = [places[m][1] * side + places[m][2] + (side * side) * places[m][0] for m in range(slots)]
    spread = [
        jnp.broadcast_to(rows[0:1, m * block : (m + 1) * block][None], shape) for m in range(slots)
    ]
    for d in range(9):
        found = jnp.zeros(shape, jnp.float32)
        for m in range(slots):
            found = found + jnp.where(inner == wanted[m] - side * side * d, spread[m], 0.0)
        part_send[d // 3, d % 3] = found
    second = begin([wide_copy(a, b) for a, b in WIDE])
    for n in range(GROUPS):
        centre_x, centre_y = centres(n)
        across = (centre_x + step_x) * (1.0 / UNIT_XY)
        aside = (centre_y + step_y) * (1.0 / UNIT_XY)
        factor = jnp.where(kind == 1, across, jnp.where(kind == 2, aside, 1.0))
        with_factor = plain_rows[n] * factor
        terms[n] = with_factor
        high, low = halves(with_factor)
        terms_pair[n, :ROWS] = high
        terms_pair[n, ROWS:] = low
    finish(goals)
    finish(second)
    for i in range(3):
        for j in range(3):
            mass = part_send[i, j]
            for a, b in WIDE:
                if 0 <= i - max(a, 0) < 3 - abs(a) and 0 <= j - max(b, 0) < 3 - abs(b):
                    mass = mass + part_recv[(a + 2) * 5 + b + 2, i, j]
            d = 3 * i + j
            mid_all[d] = dual_all[d] + step_rate * (target_all[d] - mass)

    load_duals(mid_all)
    build(True)
    pairs = []
    for n in range(GROUPS):
        inverse = invert(n)
        inverses[n] = inverse
        pairs.append(jnp.concatenate(halves(inverse), axis=0))
    total = jnp.zeros((ROWS, columns), jnp.float32)
    for n in range(GROUPS):
        masses = product(pairs[n], g_high[n], g_low[n], NN)
        depths = product(pairs[n], gz_high[n], gz_low[n], NN)
        total = total + terms[n] * jnp.where(kind == 3, depths, masses)

    def units(shape):
        which = lax.broadcasted_iota(jnp.int32, shape, 0) % 4
        unit = jnp.where(which == 0, 1.0, jnp.where(which == 3, UNIT_Z, UNIT_XY))
        return unit * (1.0 / HEAD)

    rows = fold_rows(total) * units((8, columns))
    half = lax.broadcasted_iota(jnp.int32, (8, block), 0) // 4
    for d in range(9):
        for v in range(side * side // 2):
            found = jnp.zeros((8, block), jnp.float32)
            for m in range(slots):
                here = half == wanted[m] - (side * side * d + 2 * v)
                found = found + jnp.where(here, rows[:, m * block : (m + 1) * block], 0.0)
            four_send[d, 8 * v : 8 * v + 8, :] = found
    fourth = begin([copy(3, d, four_send.at[d], four_recv) for d in AROUND])
    scale = -units((ROWS, Z))
    is_z = lax.broadcasted_iota(jnp.int32, (ROWS, Z), 0) % 4 == 3
    for n in range(GROUPS):
        across = product(terms_pair[n], g_high[n], g_low[n], NT)
        along = product(plain_pair[n], gz_high[n], gz_low[n], NT)
        offset = (inverses[n] * jnp.where(is_z, along, across)) * scale
        for r in range(2 * TY):
            for c in range(3):
                disp_ref[c, 2 * n + r // TY, r % TY : r % TY + 1, :] = offset[
                    4 * r + c + 1 : 4 * r + c + 2, :
                ]
    finish(fourth)
    four = four_send[4]
    for d in AROUND:
        four = four + four_recv[d]
    for i in range(side * side):
        r, c = i // side, i % side
        goal = target_all[4, r, c : c + 1, :]
        found = four[4 * i : 4 * i + 1]
        new_ref[r, c : c + 1, :] = mid_all[4, r, c : c + 1, :] + step_rate * (goal - found)
        weight = 1.0 / (found + goal)
        for k in range(3):
            shift_ref[k, r, c : c + 1, :] = four[4 * i + k + 1 : 4 * i + k + 2] * weight


def on_device(site_frac, dual_weight, target_mass, block_list, block_count):
    side = site_frac.shape[1]
    block = site_frac.shape[3]
    columns = block_list.shape[2] * block
    f32, bf16, i32 = jnp.float32, jnp.bfloat16, jnp.int32
    vmem = pl.BlockSpec(memory_space=pltpu.VMEM)
    place = pl.BlockSpec(memory_space=pl.ANY)
    return pl.pallas_call(
        kernel,
        out_shape=(
            pltpu.VMEM(dual_weight.shape, f32),
            pltpu.VMEM(site_frac.shape, f32),
            pltpu.VMEM((3, TX, TY, Z), f32),
        ),
        in_specs=[place] * 5,
        out_specs=(vmem, vmem, vmem),
        scratch_shapes=[
            pltpu.VMEM((9,) + site_frac.shape, f32),
            pltpu.VMEM((9,) + dual_weight.shape, f32),
            pltpu.VMEM((9,) + target_mass.shape, f32),
            pltpu.VMEM((9,) + dual_weight.shape, f32),
            pltpu.VMEM((3, 3, side, side, block), f32),
            pltpu.VMEM((25, 3, 3, side, side, block), f32),
            pltpu.VMEM((9, 4 * side * side, block), f32),
            pltpu.VMEM((9, 4 * side * side, block), f32),
            pltpu.SMEM(block_list.shape, i32),
            pltpu.SMEM(block_count.shape, i32),
            pltpu.VMEM((8, columns), f32),
            pltpu.VMEM((8, columns), f32),
            pltpu.VMEM((GROUPS, ROWS, columns), f32),
            pltpu.VMEM((GROUPS, 2 * ROWS, columns), bf16),
            pltpu.VMEM((GROUPS, ROWS, columns), f32),
            pltpu.VMEM((GROUPS, 2 * ROWS, columns), bf16),
            pltpu.VMEM((GROUPS, ROWS, Z), f32),
            pltpu.VMEM((GROUPS, Z, columns), bf16),
            pltpu.VMEM((GROUPS, Z, columns), bf16),
            pltpu.VMEM((GROUPS, Z, columns), bf16),
            pltpu.VMEM((GROUPS, Z, columns), bf16),
            pltpu.SemaphoreType.DMA((25,)),
            pltpu.SemaphoreType.DMA((25,)),
            pltpu.SemaphoreType.DMA((4, 9)),
            pltpu.SemaphoreType.DMA((4, 9)),
            pltpu.SemaphoreType.DMA((5,)),
        ],
        compiler_params=pltpu.CompilerParams(collective_id=0, has_side_effects=True),
        name="transport",
    )(site_frac, dual_weight, target_mass, block_list, block_count)


def solution(mesh):
    in_specs = (
        P(None, "gx", "gy", None),
        P("gx", "gy", None),
        P("gx", "gy", None),
        P("gx", "gy", None),
        P("gx", "gy"),
    )
    out_specs = (P("gx", "gy", None), P(None, "gx", "gy", None), P(None, "gx", "gy", None))
    return jax.shard_map(
        on_device, mesh=mesh, in_specs=in_specs, out_specs=out_specs, check_vma=False
    )
```
